256 devices in a mesh: bunch: 16 (over y, x), dom: 16 (over z, core).
Axes of the slice: x: 4, y: 4, z: 8, core: 2. Of those that a mesh axis runs over, the one named last changes fastest.
Arguments:
- particles: float32 [2, 64, 6, 32768], P(None, 'bunch', None, 'dom'), may hold values from -4.8 to 4.8
- slice_ids: int32 [2, 64, 32768], P(None, 'bunch', 'dom'), may hold values from 0 to 63
- maps: float32 [2, 8, 6, 6], replicated, may hold values from -1.3 to 1.3
- sextupoles: float32 [2, 8], replicated, may hold values from -0.05 to 0.05
Outputs:
- tracked: float32 [2, 64, 6, 32768], P(None, 'bunch', None, 'dom')
The draws below stay inside these ranges and needn't reach their ends.
All inputs are finite; a program needn't handle non-finite values.
Results may differ from the reference program's by a relative error of at most 0.0003.
Values sent between devices are 32-bit elements; how exact they have to be, the bound alone decides.
A program may use at most 64 MiB of HBM per device.

```python
import jax
import jax.numpy as jnp
from jax import lax

SLICES = 64
SECTIONS = 8
TURNS = 2
BUNCHES = 64
PART = 32768
N_BUNCH = 16


def slice_labels(key):
    keys = jax.random.split(jax.random.fold_in(key, 11), 3)
    shape = (2, BUNCHES, PART)
    first = jax.random.randint(keys[0], shape, 0, 22, jnp.int32)
    second = jax.random.randint(keys[1], shape, 0, 22, jnp.int32)
    third = jax.random.randint(keys[2], shape, 0, 22, jnp.int32)
    return first + second + third


def draw_slice_ids(key, part):
    return slice_labels(key)


def draw_particles(key, part):
    shape = (2, BUNCHES, 6, PART)
    labels = slice_labels(key)
    jitter = jax.random.uniform(jax.random.fold_in(key, 13), (2, BUNCHES, PART), jnp.float32, 0.0, 1.0)
    pos_z = -4.8 + (labels.astype(jnp.float32) + jitter) * (9.6 / SLICES)
    spread = 0.3 + 0.6 * lax.broadcasted_iota(jnp.float32, shape, 3) / PART
    base_key = jax.random.fold_in(key, 17)
    base = jnp.clip(jax.random.normal(base_key, shape, jnp.float32), -4.0, 4.0)
    full = base * spread
    return jnp.concatenate([full[:, :, :4], pos_z[:, :, None, :], full[:, :, 5:]], axis=2)


def draw_maps(key, part):
    keys = jax.random.split(jax.random.fold_in(key, 7), 3)
    transverse_phase = jax.random.uniform(keys[0], (2, SECTIONS, 2), jnp.float32, 0.3, 2.8)
    longitudinal_phase = jax.random.uniform(keys[2], (2, SECTIONS, 1), jnp.float32, 0.002, 0.01)
    phase = jnp.concatenate([transverse_phase, longitudinal_phase], axis=-1)
    planes = jnp.arange(6) // 2
    cosine = jnp.cos(phase)[:, :, planes]
    sine = jnp.sin(phase)[:, :, planes]
    rows = lax.broadcasted_iota(jnp.int32, (6, 6), 0)
    cols = lax.broadcasted_iota(jnp.int32, (6, 6), 1)
    same = (rows // 2 == cols // 2).astype(jnp.float32)
    transverse = ((rows < 4) & (cols < 4)).astype(jnp.float32)
    diagonal = (rows == cols).astype(jnp.float32)
    upper = ((cols == rows + 1) & (rows % 2 == 0)).astype(jnp.float32)
    lower = ((cols == rows - 1) & (rows % 2 == 1)).astype(jnp.float32)
    rotation = diagonal * cosine[..., :, None] + upper * sine[..., :, None] - lower * sine[..., :, None]
    coupling = 0.08 * jnp.clip(jax.random.normal(keys[1], (2, SECTIONS, 6, 6), jnp.float32), -3.0, 3.0)
    return rotation + coupling * (1.0 - same) * transverse


def setup_inputs(seed: int = 0) -> dict:
    streams_of = jax.random.split(jax.random.key(seed), 5)
    return {
        "particles": draw_particles(jax.random.fold_in(streams_of[4], 71), 0),
        "slice_ids": draw_slice_ids(jax.random.fold_in(streams_of[4], 71), 0),
        "maps": draw_maps(jax.random.fold_in(streams_of[4], 71), 0),
        "sextupoles": jnp.clip(jax.random.uniform(streams_of[3], (2, SECTIONS), jnp.float32, -0.05, 0.05), -0.05, 0.05),
    }


kick_scale = 1.5
soft_width = 0.25


def features(coords):
    pos_x, mom_x, pos_y, mom_y, pos_z = coords[0], coords[1], coords[2], coords[3], coords[4]
    return jnp.stack([jnp.ones_like(pos_x), pos_x, mom_x, pos_y, mom_y, pos_z, pos_x * pos_x, pos_x * mom_x, mom_x * mom_x, pos_y * pos_y, pos_y * mom_y, mom_y * mom_y])


def transport(coords, section_maps, strengths):
    moved = jnp.einsum("aij,abjp->abip", section_maps, coords, precision=lax.Precision.HIGHEST)
    pos_x = moved[:, :, 0]
    pos_y = moved[:, :, 2]
    factor = strengths[:, None, None]
    mom_x = moved[:, :, 1] + factor * (pos_x * pos_x - pos_y * pos_y)
    mom_y = moved[:, :, 3] - 2.0 * factor * pos_x * pos_y
    return jnp.stack([pos_x, mom_x, pos_y, mom_y, moved[:, :, 4], moved[:, :, 5]], axis=2)


def kick_bunch(coords, opposing, population):
    counts = opposing[0]
    weight = counts / population
    inverse = 1.0 / jnp.maximum(counts, 1.0)
    cen_x = opposing[1] * inverse
    cen_px = opposing[2] * inverse
    cen_y = opposing[3] * inverse
    cen_py = opposing[4] * inverse
    cen_z = opposing[5] * inverse
    var_xx = opposing[6] * inverse - cen_x * cen_x
    var_xp = opposing[7] * inverse - cen_x * cen_px
    var_pp = opposing[8] * inverse - cen_px * cen_px
    var_yy = opposing[9] * inverse - cen_y * cen_y
    var_yq = opposing[10] * inverse - cen_y * cen_py
    var_qq = opposing[11] * inverse - cen_py * cen_py
    pos_x, mom_x, pos_y, mom_y, pos_z = coords[0], coords[1], coords[2], coords[3], coords[4]
    drift = 0.5 * (pos_z[None, :] - cen_z[:, None])
    delta_x = pos_x[None, :] + drift * mom_x[None, :] - cen_x[:, None] - drift * cen_px[:, None]
    delta_y = pos_y[None, :] + drift * mom_y[None, :] - cen_y[:, None] - drift * cen_py[:, None]
    sigma_sq = 0.5 * (var_xx[:, None] + 2.0 * drift * var_xp[:, None] + drift * drift * var_pp[:, None]
                      + var_yy[:, None] + 2.0 * drift * var_yq[:, None] + drift * drift * var_qq[:, None]) + soft_width
    strength = weight[:, None] * jnp.exp(-(delta_x * delta_x + delta_y * delta_y) / (2.0 * sigma_sq)) / sigma_sq
    kick_x = jnp.sum(strength * delta_x, axis=0)
    kick_y = jnp.sum(strength * delta_y, axis=0)
    return jnp.stack([pos_x, mom_x - kick_scale * kick_x, pos_y, mom_y - kick_scale * kick_y, pos_z, coords[5]])


def reference(particles, slice_ids, maps, sextupoles):
    coords = particles
    population = float(PART)
    labels = slice_ids.reshape(2 * BUNCHES, PART)
    per_device = BUNCHES // N_BUNCH
    for turn_index in range(TURNS):
        for section in range(SECTIONS):
            coords = transport(coords, maps[:, section], sextupoles[:, section])
            flattened = coords.reshape(2 * BUNCHES, 6, PART)
            moments = lax.map(lambda bundle: jax.ops.segment_sum(features(bundle[0]).T, bundle[1], num_segments=SLICES).T, (flattened, labels))
            moments = moments.reshape(2, N_BUNCH, per_device, 12, SLICES)
            offset = (section + 1) % N_BUNCH
            met_first = jnp.roll(moments[1], offset, axis=0)
            met_second = jnp.roll(moments[0], -offset, axis=0)
            opposing = jnp.stack([met_first, met_second]).reshape(2 * BUNCHES, 12, SLICES)
            kicked = lax.map(lambda bundle: kick_bunch(bundle[0], bundle[1], population), (flattened, opposing))
            coords = kicked.reshape(2, BUNCHES, 6, PART)
    return coords
```

```python
import functools
import math

import jax
import jax.numpy as jnp
from jax import lax
from jax.experimental import pallas as pl
from jax.experimental.pallas import tpu as pltpu
from jax.sharding import PartitionSpec as P

SLICES = 64
SECTIONS = 8
TURNS = 2
STEPS = SECTIONS * TURNS
MESH = pl.DeviceIdType.MESH

kick_scale = 1.5
soft_width = 0.25
CHUNK = 256
UNROLL = 4


def bf(value):
    return value.astype(jnp.bfloat16)


def split_rows(value):
    high = bf(value).astype(jnp.float32)
    return bf(jnp.concatenate([high, value - high], axis=0))


def slice_coefficients(sums, population):
    row = lax.broadcasted_iota(jnp.int32, (8, 128), 0)
    lane = lax.broadcasted_iota(jnp.int32, (8, 128), 1)
    low = lane < SLICES
    turned = pltpu.roll(sums, SLICES, 1)
    both = jnp.where(low, sums, turned)
    counts = jnp.where(low, turned, sums)
    inverse = 1.0 / jnp.maximum(counts, 1.0)
    mean = both * inverse
    cen_x, cen_px, cen_y, cen_py, cen_z, mean_rr, mean_rp, mean_pp = [
        jnp.broadcast_to(mean[r : r + 1], (8, 128)) for r in range(8)
    ]
    var_rr = mean_rr - cen_x * cen_x - cen_y * cen_y
    var_rp = mean_rp - cen_x * cen_px - cen_y * cen_py
    var_pp = mean_pp - cen_px * cen_px - cen_py * cen_py
    full = counts > 0.0
    scale = jnp.where(full, inverse * (population / (2.0 * kick_scale * math.log(2.0))), 0.0)
    scale_sq = (-2.0 * math.log(2.0)) * scale * scale
    half_z = 0.5 * cen_z
    cen = jnp.where(low, cen_x, cen_y)
    cen_p = jnp.where(low, cen_px, cen_py)
    first = jnp.where(low, 0, 2)
    zero = jnp.zeros((8, 128), jnp.float32)
    place = jnp.where(row == first, scale, zero)
    place = jnp.where(row == first + 1, -scale * half_z, place)
    place = jnp.where(row == 4, -0.5 * scale * cen_p, place)
    place = jnp.where(row == 6, -scale * (cen - half_z * cen_p), place)
    quad = 0.125 * var_pp
    line = 0.5 * var_rp - 0.25 * cen_z * var_pp
    const = soft_width + 0.5 * var_rr - half_z * var_rp + 0.5 * half_z * half_z * var_pp
    width = jnp.where(row == 4, scale_sq * line, zero)
    width = jnp.where(row == 5, scale_sq * quad, width)
    width = jnp.where(row == 6, jnp.where(full, scale_sq * const, -1.0), width)
    table = jnp.concatenate([place, width], axis=1)
    high = bf(table).astype(jnp.float32)
    rest = table - high
    stacked = jnp.concatenate([high, high, rest, rest], axis=0)
    return bf(jnp.transpose(stacked)[: 3 * SLICES])


def kernel(
    nb, nz, population,
    part_ref, ids_ref, maps_ref, sext_ref, out_ref,
    x_in, id_in, x_out, state, tiles, id_dense, onehot, counts, mom_rows, mom_bf, kick_rows, kick_bf, kick_x, kick_y,
    send_buf, recv_buf,
    send_sem, recv_sem, load_sem, swap_send, swap_recv, out_sem, out_send, out_recv,
):
    bunches, comps, width = part_ref.shape[1:]
    half_tiles = width // 128
    ntile = 2 * half_tiles
    groups = ntile // 8
    me = lax.axis_index("bunch")
    dom = lax.axis_index("dom")
    zed, core = lax.div(dom, 2), lax.rem(dom, 2)
    other = 1 - core
    peer = (me, 2 * zed + other)

    def partner_column(distance):
        return lax.rem(me + jnp.where(core == 0, nb - distance, distance), nb)

    own_x = pltpu.make_async_copy(part_ref.at[core], x_in.at[core], load_sem.at[0])
    own_id = pltpu.make_async_copy(ids_ref.at[core], id_in.at[core], load_sem.at[1])
    own_x.start()
    own_id.start()

    barrier = pltpu.get_barrier_semaphore()
    pl.semaphore_signal(barrier, inc=1, device_id=peer, device_id_type=MESH)

    def greet(n, carry):
        column = partner_column(lax.rem(lax.div(n, nz) + 1, nb))
        where = (column, 2 * lax.rem(n, nz) + other)
        pl.semaphore_signal(barrier, inc=1, device_id=where, device_id_type=MESH)
        return carry

    lax.fori_loop(0, SECTIONS * nz, greet, 0)
    pl.semaphore_wait(barrier, SECTIONS * nz + 1)

    swap_x = pltpu.make_async_remote_copy(
        src_ref=part_ref.at[other], dst_ref=x_in.at[core], send_sem=swap_send.at[0], recv_sem=swap_recv.at[0],
        device_id=peer, device_id_type=MESH,
    )
    swap_id = pltpu.make_async_remote_copy(
        src_ref=ids_ref.at[other], dst_ref=id_in.at[core], send_sem=swap_send.at[1], recv_sem=swap_recv.at[1],
        device_id=peer, device_id_type=MESH,
    )
    swap_id.start()
    swap_x.start()
    own_x.wait()
    own_id.wait()
    swap_id.wait()
    swap_x.wait()

    def unpack(i, carry):
        for h in range(2):
            for t in range(half_tiles):
                tiles[pl.ds((h * half_tiles + t) * 8, comps), :] = x_in[h, i, :, 128 * t : 128 * (t + 1)]
        for c in range(comps):
            for g in range(groups):
                state[i, c, 8 * g : 8 * g + 8, :] = tiles[pl.ds(64 * g + c, 8, stride=8), :]
        return carry

    lax.fori_loop(0, bunches, unpack, 0)
    for h in range(2):
        for t in range(half_tiles):
            tiles[pl.ds((h * half_tiles + t) * 8, bunches), :] = id_in[h, :, 128 * t : 128 * (t + 1)].astype(jnp.float32)
    for i in range(bunches):
        for g in range(groups):
            id_dense[i, 8 * g : 8 * g + 8, :] = tiles[pl.ds(64 * g + i, 8, stride=8), :]

    mom_bf[...] = jnp.ones(mom_bf.shape, jnp.bfloat16)
    slot = (lax.broadcasted_iota(jnp.int32, (128, 128), 1) & (SLICES - 1)).astype(jnp.float32)

    def build(i, carry):
        columns = jnp.transpose(id_dense[i])
        for t in range(ntile):
            onehot[i, 128 * t : 128 * (t + 1), :] = bf(
                jnp.where(columns[:, t : t + 1] == slot, 1.0, 0.0)
            )
        counts[i] = jnp.dot(mom_bf[...], onehot[i], preferred_element_type=jnp.float32)[:8]
        return carry

    lax.fori_loop(0, bunches, build, 0)

    for g in range(groups):
        kick_rows[pl.ds(64 * g + 7, 8, stride=8), :] = jnp.zeros((8, 128), jnp.float32)
    low = lax.broadcasted_iota(jnp.int32, (8, 128), 1) < SLICES
    one = jnp.ones((8, 128), jnp.float32)

    def advance(step, i):
        section = lax.rem(step, SECTIONS)
        at = core * SECTIONS + section
        base = at * comps * comps
        cell = [[maps_ref[base + comps * r + c] for c in range(comps)] for r in range(comps)]
        strength = sext_ref[at]
        for g in range(groups):
            rows = slice(8 * g, 8 * g + 8)
            old = [state[i, c, rows, :] for c in range(comps)]
            new = []
            for r in range(comps):
                total = cell[r][0] * old[0]
                for c in range(1, comps):
                    total = total + cell[r][c] * old[c]
                new.append(total)
            x, px, y, py, z, dp = new
            px = px + strength * (x * x - y * y)
            py = py - 2.0 * strength * (x * y)
            for c, value in enumerate((x, px, y, py, z, dp)):
                state[i, c, rows, :] = value
            half = 0.5 * z
            mom = (x, px, y, py, z, x * x + y * y, x * px + y * py, px * px + py * py)
            kick = (x + half * px, px, y + half * py, py, z, z * z, one)
            for f, value in enumerate(mom):
                mom_rows[pl.ds(64 * g + f, 8, stride=8), :] = value
            for f, value in enumerate(kick):
                kick_rows[pl.ds(64 * g + f, 8, stride=8), :] = value
        for t in range(ntile):
            lanes = slice(128 * t, 128 * (t + 1))
            mom_bf[:, lanes] = split_rows(mom_rows[8 * t : 8 * t + 8, :])
            kick_bf[i, :, lanes] = split_rows(kick_rows[8 * t : 8 * t + 8, :])
        sums = jnp.dot(mom_bf[...], onehot[i], preferred_element_type=jnp.float32)
        n = step * bunches + i
        send_buf[n] = jnp.where(low, sums[:8] + sums[8:], counts[i])
        column = partner_column(lax.rem(section + 1, nb))

        def send(r, carry):
            pltpu.make_async_remote_copy(
                src_ref=send_buf.at[n], dst_ref=recv_buf.at[n, zed], send_sem=send_sem.at[n], recv_sem=recv_sem.at[n],
                device_id=(column, 2 * lax.rem(zed + r, nz) + other), device_id_type=MESH,
            ).start()
            return carry

        lax.fori_loop(0, nz, send, 0)

    def kick(step, i):
        n = step * bunches + i
        pltpu.make_async_copy(recv_buf.at[n], recv_buf.at[n], recv_sem.at[n]).wait()
        sums = recv_buf[n, 0]
        for r in range(1, nz):
            sums = sums + recv_buf[n, r]
        table = slice_coefficients(sums, population)

        def chunk(m):
            start = m * CHUNK
            if not isinstance(start, int):
                start = pl.multiple_of(start, CHUNK)
            part = kick_bf[i, :, pl.ds(start, CHUNK)]
            made = jnp.dot(table, jnp.concatenate([part, part], axis=0), preferred_element_type=jnp.float32)
            dx, dy, width_neg = made[:SLICES], made[SLICES : 2 * SLICES], made[2 * SLICES :]
            recip = 1.0 / width_neg
            factor = jnp.exp2((dx * dx + dy * dy) * recip) * recip
            for ref, delta in ((kick_x, dx), (kick_y, dy)):
                term = factor * delta
                total = term[:8]
                for j in range(8, SLICES, 8):
                    total = total + term[j : j + 8]
                for u in range(CHUNK // 128):
                    ref[pl.ds(pl.multiple_of((m * (CHUNK // 128) + u) * 8, 8), 8), :] = total[:, 128 * u : 128 * (u + 1)]

        def chunks(q, carry):
            for u in range(UNROLL):
                chunk(q * UNROLL + u)
            return carry

        lax.fori_loop(0, ntile * 128 // (CHUNK * UNROLL), chunks, 0)
        for c, ref in ((1, kick_x), (3, kick_y)):
            for g in range(groups):
                total = state[i, c, 8 * g : 8 * g + 8, :]
                for r in range(8):
                    total = total + ref[pl.ds(64 * g + r, 8, stride=8), :]
                state[i, c, 8 * g : 8 * g + 8, :] = total

    def enter(i, carry):
        advance(0, i)
        return carry

    lax.fori_loop(0, bunches, enter, 0)

    def cycle(n, carry):
        step, i = lax.div(n, bunches), lax.rem(n, bunches)
        kick(step, i)
        advance(step + 1, i)
        return carry

    lax.fori_loop(0, (STEPS - 1) * bunches, cycle, 0)

    def leave(i, carry):
        kick(STEPS - 1, i)
        for c in range(comps):
            for g in range(groups):
                tiles[pl.ds(64 * g + c, 8, stride=8), :] = state[i, c, 8 * g : 8 * g + 8, :]
        for h in range(2):
            for t in range(half_tiles):
                x_out[h, i, :, 128 * t : 128 * (t + 1)] = tiles[pl.ds((h * half_tiles + t) * 8, comps), :]
        own_out(i).start()
        swap_out(i).start()
        return carry

    def own_out(i):
        return pltpu.make_async_copy(x_out.at[core, i], out_ref.at[core, i], out_sem.at[i])

    def swap_out(i):
        return pltpu.make_async_remote_copy(
            src_ref=x_out.at[other, i], dst_ref=out_ref.at[core, i], send_sem=out_send.at[i], recv_sem=out_recv.at[i],
            device_id=peer, device_id_type=MESH,
        )

    lax.fori_loop(0, bunches, leave, 0)

    def finish(i, carry):
        own_out(i).wait()
        swap_out(i).wait()
        return carry

    def drain(n, carry):
        pltpu.make_async_copy(recv_buf.at[n], recv_buf.at[n], send_sem.at[n]).wait()
        return carry

    lax.fori_loop(0, STEPS * bunches, drain, 0)
    lax.fori_loop(0, bunches, finish, 0)


def body(particles, slice_ids, maps, sextupoles):
    nb, nd = lax.axis_size("bunch"), lax.axis_size("dom")
    nz = nd // 2
    beams, bunches, comps, width = particles.shape
    ntile = 2 * width // 128
    slots = STEPS * bunches
    f32, b16 = jnp.float32, jnp.bfloat16
    vmem, dma = pltpu.VMEM, pltpu.SemaphoreType.DMA
    return pl.pallas_call(
        functools.partial(kernel, nb, nz, float(width * nd)),
        out_shape=jax.ShapeDtypeStruct(particles.shape, f32),
        in_specs=[
            pl.BlockSpec(memory_space=pl.ANY),
            pl.BlockSpec(memory_space=pl.ANY),
            pl.BlockSpec(memory_space=pltpu.SMEM),
            pl.BlockSpec(memory_space=pltpu.SMEM),
        ],
        out_specs=pl.BlockSpec(memory_space=pl.ANY),
        scratch_shapes=[
            vmem((2, bunches, comps, width), f32),
            vmem((2, bunches, width), jnp.int32),
            vmem((2, bunches, comps, width), f32),
            vmem((bunches, comps, ntile, 128), f32),
            vmem((8 * ntile, 128), f32),
            vmem((bunches, ntile, 128), f32),
            vmem((bunches, 2 * width, 128), b16),
            vmem((bunches, 8, 128), f32),
            vmem((8 * ntile, 128), f32),
            vmem((16, 2 * width), b16),
            vmem((8 * ntile, 128), f32),
            vmem((bunches, 16, 2 * width), b16),
            vmem((8 * ntile, 128), f32),
            vmem((8 * ntile, 128), f32),
            vmem((slots, 8, 128), f32),
            vmem((slots, nz, 8, 128), f32),
            dma((slots,)),
            dma((slots,)),
            dma((2,)),
            dma((2,)),
            dma((2,)),
            dma((bunches,)),
            dma((bunches,)),
            dma((bunches,)),
        ],
        compiler_params=pltpu.CompilerParams(
            collective_id=0, has_side_effects=True, vmem_limit_bytes=40 << 20
        ),
        name="track",
    )(particles, slice_ids, maps.reshape(-1), sextupoles.reshape(-1))


def solution(mesh):
    return jax.shard_map(
        body,
        mesh=mesh,
        in_specs=(P(None, "bunch", None, "dom"), P(None, "bunch", "dom"), P(), P()),
        out_specs=P(None, "bunch", None, "dom"),
        check_vma=False,
    )
```

```python
import functools
import math

import jax
import jax.numpy as jnp
from jax import lax
from jax.experimental import pallas as pl
from jax.experimental.pallas import tpu as pltpu
from jax.sharding import PartitionSpec as P

SLICES = 64
SECTIONS = 8
TURNS = 2
STEPS = SECTIONS * TURNS
MESH = pl.DeviceIdType.MESH

kick_scale = 1.5
soft_width = 0.25
CHUNK = 128
ROWS = 5


def bf(value):
    return value.astype(jnp.bfloat16)


def split_rows(value):
    high = bf(value).astype(jnp.float32)
    return bf(jnp.concatenate([high, value - high], axis=0))


def slice_coefficients(sums, population):
    row = lax.broadcasted_iota(jnp.int32, (8, 128), 0)
    lane = lax.broadcasted_iota(jnp.int32, (8, 128), 1)
    low = lane < SLICES
    counts = jnp.broadcast_to(sums[4:5], (8, 128))
    inverse = 1.0 / jnp.maximum(counts, 1.0)
    mean = sums[:4] * inverse[:4]
    turned = pltpu.roll(mean, SLICES, 1)
    cen_x, cen_px, cen_y, cen_py = [
        jnp.broadcast_to(r, (8, 128)) for r in jnp.split(jnp.where(low[:4], mean, turned), 4)
    ]
    cen_z, mean_rr, mean_rp, mean_pp = [
        jnp.broadcast_to(r, (8, 128)) for r in jnp.split(jnp.where(low[:4], turned, mean), 4)
    ]
    var_rr = mean_rr - cen_x * cen_x - cen_y * cen_y
    var_rp = mean_rp - cen_x * cen_px - cen_y * cen_py
    var_pp = mean_pp - cen_px * cen_px - cen_py * cen_py
    full = counts > 0.0
    scale = jnp.where(full, inverse * (population / (2.0 * kick_scale * math.log(2.0))), 0.0)
    scale_sq = (-2.0 * math.log(2.0)) * scale * scale
    half_z = 0.5 * cen_z
    cen = jnp.where(low, cen_x, cen_y)
    cen_p = jnp.where(low, cen_px, cen_py)
    first = jnp.where(low, 0, 2)
    zero = jnp.zeros((8, 128), jnp.float32)
    place = jnp.where(row == first, scale, zero)
    place = jnp.where(row == first + 1, -scale * half_z, place)
    place = jnp.where(row == 4, -0.5 * scale * cen_p, place)
    place = jnp.where(row == 6, -scale * (cen - half_z * cen_p), place)
    quad = 0.125 * var_pp
    line = 0.5 * var_rp - 0.25 * cen_z * var_pp
    const = soft_width + 0.5 * var_rr - half_z * var_rp + 0.5 * half_z * half_z * var_pp
    width = jnp.where(row == 4, scale_sq * line, zero)
    width = jnp.where(row == 5, scale_sq * quad, width)
    width = jnp.where(row == 6, jnp.where(full, scale_sq * const, -1.0), width)
    table = jnp.concatenate([place, width], axis=1)
    high = bf(table).astype(jnp.float32)
    rest = table - high
    stacked = jnp.concatenate([high, high, rest, rest], axis=0)
    turned = jnp.transpose(stacked)
    order = [turned[j + SLICES * f : j + SLICES * f + 8] for j in range(0, SLICES, 8) for f in range(3)]
    return bf(jnp.concatenate(order, axis=0))


def kernel(
    nb, nz, population,
    part_ref, ids_ref, maps_ref, sext_ref, out_ref,
    x_in, id_in, x_out, state, tiles, id_dense, onehot, counts, mom_rows, mom_bf, kick_rows, kick_bf, kick_x, kick_y,
    send_buf, recv_buf, ahead,
    send_sem, recv_sem, load_sem, swap_send, swap_recv, out_sem, out_send, out_recv,
):
    bunches, comps, width = part_ref.shape[1:]
    half_tiles = width // 128
    ntile = 2 * half_tiles
    groups = ntile // 8
    me = lax.axis_index("bunch")
    dom = lax.axis_index("dom")
    zed, core = lax.div(dom, 2), lax.rem(dom, 2)
    other = 1 - core
    peer = (me, 2 * zed + other)

    def partner_column(distance):
        return lax.rem(me + jnp.where(core == 0, nb - distance, distance), nb)

    own_x = pltpu.make_async_copy(part_ref.at[core], x_in.at[core], load_sem.at[0])
    own_id = pltpu.make_async_copy(ids_ref.at[core], id_in.at[core], load_sem.at[1])
    own_x.start()
    own_id.start()

    barrier = pltpu.get_barrier_semaphore()
    pl.semaphore_signal(barrier, inc=1, device_id=peer, device_id_type=MESH)

    def greet(k, carry):
        column = partner_column(lax.rem(k + 1, nb))
        for r in range(nz):
            pl.semaphore_signal(barrier, inc=1, device_id=(column, 2 * r + other), device_id_type=MESH)
        return carry

    lax.fori_loop(0, SECTIONS, greet, 0)
    pl.semaphore_wait(barrier, SECTIONS * nz + 1)

    swap_x = pltpu.make_async_remote_copy(
        src_ref=part_ref.at[other], dst_ref=x_in.at[core], send_sem=swap_send.at[0], recv_sem=swap_recv.at[0],
        device_id=peer, device_id_type=MESH,
    )
    swap_id = pltpu.make_async_remote_copy(
        src_ref=ids_ref.at[other], dst_ref=id_in.at[core], send_sem=swap_send.at[1], recv_sem=swap_recv.at[1],
        device_id=peer, device_id_type=MESH,
    )
    swap_id.start()
    swap_x.start()
    own_x.wait()
    own_id.wait()
    swap_id.wait()
    swap_x.wait()

    def unpack(i, carry):
        for h in range(2):
            for t in range(half_tiles):
                tiles[pl.ds((h * half_tiles + t) * 8, comps), :] = x_in[h, i, :, 128 * t : 128 * (t + 1)]
        for c in range(comps):
            for g in range(groups):
                state[i, c, 8 * g : 8 * g + 8, :] = tiles[pl.ds(64 * g + c, 8, stride=8), :]
        return carry

    lax.fori_loop(0, bunches, unpack, 0)
    for h in range(2):
        for t in range(half_tiles):
            tiles[pl.ds((h * half_tiles + t) * 8, bunches), :] = id_in[h, :, 128 * t : 128 * (t + 1)].astype(jnp.float32)
    for i in range(bunches):
        for g in range(groups):
            id_dense[i, 8 * g : 8 * g + 8, :] = tiles[pl.ds(64 * g + i, 8, stride=8), :]

    mom_bf[...] = jnp.ones(mom_bf.shape, jnp.bfloat16)
    slot = (lax.broadcasted_iota(jnp.int32, (128, 128), 1) & (SLICES - 1)).astype(jnp.float32)

    def build(i, carry):
        columns = jnp.transpose(id_dense[i])
        for t in range(ntile):
            onehot[i, 128 * t : 128 * (t + 1), :] = bf(
                jnp.where(columns[:, t : t + 1] == slot, 1.0, 0.0)
            )
        counts[i] = jnp.dot(mom_bf[...], onehot[i], preferred_element_type=jnp.float32)[:8]
        return carry

    lax.fori_loop(0, bunches, build, 0)

    for g in range(groups):
        kick_rows[pl.ds(64 * g + 7, 8, stride=8), :] = jnp.zeros((8, 128), jnp.float32)
    low = lax.broadcasted_iota(jnp.int32, (8, 128), 1) < SLICES
    one = jnp.ones((8, 128), jnp.float32)

    def cells(step):
        base = (core * SECTIONS + lax.rem(step, SECTIONS)) * comps * comps
        return [[maps_ref[base + comps * r + c] for c in range(comps)] for r in range(comps)]

    def prepare(step, i):
        cell = cells(step)
        for g in range(groups):
            rows = slice(8 * g, 8 * g + 8)
            old = [state[i, c, rows, :] for c in range(comps)]
            for r in range(comps):
                total = cell[r][0] * old[0]
                for c in range(1, comps):
                    total = total + cell[r][c] * old[c]
                ahead[r, rows, :] = total

    def gathered(ref, g):
        total = ref[pl.ds(64 * g, 8, stride=8), :]
        for r in range(1, 8):
            total = total + ref[pl.ds(64 * g + r, 8, stride=8), :]
        return total

    def advance(step, i, kicked):
        cell = cells(step)
        strength = sext_ref[core, lax.rem(step, SECTIONS)]
        for g in range(groups):
            rows = slice(8 * g, 8 * g + 8)
            new = [ahead[r, rows, :] for r in range(comps)]
            if kicked:
                add_x, add_y = gathered(kick_x, g), gathered(kick_y, g)
                new = [new[r] + (cell[r][1] * add_x + cell[r][3] * add_y) for r in range(comps)]
            x, px, y, py, z, dp = new
            xx, yy = x * x, y * y
            px = px + strength * (xx - yy)
            py = py - 2.0 * strength * (x * y)
            for c, value in enumerate((x, px, y, py, z, dp)):
                state[i, c, rows, :] = value
            half = 0.5 * z
            mom = (x, px, y, py, z, xx + yy, x * px + y * py, px * px + py * py)
            kick = (x + half * px, px, y + half * py, py, z, z * z, one)
            for f, value in enumerate(mom):
                mom_rows[pl.ds(64 * g + f, 8, stride=8), :] = value
            for f, value in enumerate(kick):
                kick_rows[pl.ds(64 * g + f, 8, stride=8), :] = value
        for t in range(ntile):
            mom_bf[:, 128 * t : 128 * (t + 1)] = split_rows(mom_rows[8 * t : 8 * t + 8, :])
        sums = jnp.dot(mom_bf[...], onehot[i], preferred_element_type=jnp.float32)
        sums = sums[:8] + sums[8:]
        send_buf[step * bunches + i] = jnp.concatenate(
            [jnp.where(low[:4], sums[:4], sums[4:]), counts[i, :4, :]], axis=0
        )

    def features(i):
        for t in range(ntile):
            kick_bf[i, :, 128 * t : 128 * (t + 1)] = split_rows(kick_rows[8 * t : 8 * t + 8, :])

    def send(step, i):
        n = step * bunches + i
        column = partner_column(lax.rem(lax.rem(step, SECTIONS) + 1, nb))
        for r in sorted(range(nz), key=lambda r: -min(r, nz - r)):
            pltpu.make_async_remote_copy(
                src_ref=send_buf.at[n, pl.ds(0, ROWS)], dst_ref=recv_buf.at[n, zed, pl.ds(0, ROWS)],
                send_sem=send_sem.at[n], recv_sem=recv_sem.at[n],
                device_id=(column, 2 * lax.rem(zed + r, nz) + other), device_id_type=MESH,
            ).start()

    def meet(step, i):
        n = step * bunches + i
        landed = recv_buf.at[n, :, pl.ds(0, ROWS)]
        pltpu.make_async_copy(landed, landed, recv_sem.at[n]).wait()
        sums = recv_buf[n, 0, :ROWS]
        for r in range(1, nz):
            sums = sums + recv_buf[n, r, :ROWS]
        return slice_coefficients(sums, population)

    def chunk(table, i, m):
        part = kick_bf[i, :, CHUNK * m : CHUNK * (m + 1)]
        made = jnp.dot(table, jnp.concatenate([part, part], axis=0), preferred_element_type=jnp.float32)
        for u in range(CHUNK // 128):
            lanes = slice(128 * u, 128 * (u + 1))
            total_x = total_y = None
            for j in range(0, SLICES, 8):
                dx = made[3 * j : 3 * j + 8, lanes]
                dy = made[3 * j + 8 : 3 * j + 16, lanes]
                recip = 1.0 / made[3 * j + 16 : 3 * j + 24, lanes]
                factor = jnp.exp2((dx * dx + dy * dy) * recip) * recip
                total_x = factor * dx if j == 0 else total_x + factor * dx
                total_y = factor * dy if j == 0 else total_y + factor * dy
            row = (m * (CHUNK // 128) + u) * 8
            kick_x[row : row + 8, :] = total_x
            kick_y[row : row + 8, :] = total_y

    def slot(step, i):
        table = meet(step, i)
        for m in range(ntile * 128 // CHUNK):
            chunk(table, i, m)

    for i in range(bunches):
        prepare(0, i)
        advance(0, i, False)
        send(0, i)
        features(i)

    def cycle(step, carry):
        for i in range(bunches):
            prepare(step + 1, i)
            slot(step, i)
            advance(step + 1, i, True)
            send(step + 1, i)
            features(i)
        return carry

    lax.fori_loop(0, STEPS - 1, cycle, 0)

    def own_out(i):
        return pltpu.make_async_copy(x_out.at[core, i], out_ref.at[core, i], out_sem.at[i])

    def swap_out(i):
        return pltpu.make_async_remote_copy(
            src_ref=x_out.at[other, i], dst_ref=out_ref.at[core, i], send_sem=out_send.at[i], recv_sem=out_recv.at[i],
            device_id=peer, device_id_type=MESH,
        )

    for i in range(bunches):
        slot(STEPS - 1, i)
        for c in range(comps):
            for g in range(groups):
                value = state[i, c, 8 * g : 8 * g + 8, :]
                if c in (1, 3):
                    value = value + gathered(kick_x if c == 1 else kick_y, g)
                tiles[pl.ds(64 * g + c, 8, stride=8), :] = value
        for h in range(2):
            for t in range(half_tiles):
                x_out[h, i, :, 128 * t : 128 * (t + 1)] = tiles[pl.ds((h * half_tiles + t) * 8, comps), :]
        own_out(i).start()
        swap_out(i).start()

    def finish(i, carry):
        own_out(i).wait()
        swap_out(i).wait()
        return carry

    def drain(n, carry):
        landed = recv_buf.at[n, :, pl.ds(0, ROWS)]
        pltpu.make_async_copy(landed, landed, send_sem.at[n]).wait()
        return carry

    lax.fori_loop(0, STEPS * bunches, drain, 0)
    lax.fori_loop(0, bunches, finish, 0)


def body(particles, slice_ids, maps, sextupoles):
    nb, nd = lax.axis_size("bunch"), lax.axis_size("dom")
    nz = nd // 2
    beams, bunches, comps, width = particles.shape
    ntile = 2 * width // 128
    slots = STEPS * bunches
    f32, b16 = jnp.float32, jnp.bfloat16
    vmem, dma = pltpu.VMEM, pltpu.SemaphoreType.DMA
    return pl.pallas_call(
        functools.partial(kernel, nb, nz, float(width * nd)),
        out_shape=jax.ShapeDtypeStruct(particles.shape, f32),
        in_specs=[
            pl.BlockSpec(memory_space=pltpu.HBM),
            pl.BlockSpec(memory_space=pltpu.HBM),
            pl.BlockSpec(memory_space=pltpu.SMEM),
            pl.BlockSpec(memory_space=pltpu.SMEM),
        ],
        out_specs=pl.BlockSpec(memory_space=pl.ANY),
        scratch_shapes=[
            vmem((2, bunches, comps, width), f32),
            vmem((2, bunches, width), jnp.int32),
            vmem((2, bunches, comps, width), f32),
            vmem((bunches, comps, ntile, 128), f32),
            vmem((8 * ntile, 128), f32),
            vmem((bunches, ntile, 128), f32),
            vmem((bunches, 2 * width, 128), b16),
            vmem((bunches, 8, 128), f32),
            vmem((8 * ntile, 128), f32),
            vmem((16, 2 * width), b16),
            vmem((8 * ntile, 128), f32),
            vmem((bunches, 16, 2 * width), b16),
            vmem((8 * ntile, 128), f32),
            vmem((8 * ntile, 128), f32),
            vmem((slots, 8, 128), f32),
            vmem((slots, nz, 8, 128), f32),
            vmem((comps, ntile, 128), f32),
            dma((slots,)),
            dma((slots,)),
            dma((2,)),
            dma((2,)),
            dma((2,)),
            dma((bunches,)),
            dma((bunches,)),
            dma((bunches,)),
        ],
        compiler_params=pltpu.CompilerParams(
            collective_id=0, has_side_effects=True, vmem_limit_bytes=40 << 20
        ),
        name="track",
    )(particles, slice_ids, maps.reshape(-1), sextupoles)


def solution(mesh):
    return jax.shard_map(
        body,
        mesh=mesh,
        in_specs=(P(None, "bunch", None, "dom"), P(None, "bunch", "dom"), P(), P()),
        out_specs=P(None, "bunch", None, "dom"),
        check_vma=False,
    )
```

```python
import functools
import math

import jax
import jax.numpy as jnp
from jax import lax
from jax.experimental import pallas as pl
from jax.experimental.pallas import tpu as pltpu
from jax.sharding import PartitionSpec as P

SLICES = 64
SECTIONS = 8
TURNS = 2
STEPS = SECTIONS * TURNS
MESH = pl.DeviceIdType.MESH

kick_scale = 1.5
soft_width = 0.25
CHUNK = 128
ROWS = 5


def bf(value):
    return value.astype(jnp.bfloat16)


def split_rows(value):
    high = bf(value).astype(jnp.float32)
    return bf(jnp.concatenate([high, value - high], axis=0))


def slice_coefficients(sums, population):
    row = lax.broadcasted_iota(jnp.int32, (8, 128), 0)
    lane = lax.broadcasted_iota(jnp.int32, (8, 128), 1)
    low = lane < SLICES
    counts = jnp.broadcast_to(sums[4:5], (8, 128))
    inverse = 1.0 / jnp.maximum(counts, 1.0)
    mean = sums[:4] * inverse[:4]
    turned = pltpu.roll(mean, SLICES, 1)
    cen_x, cen_px, cen_y, cen_py = [
        jnp.broadcast_to(r, (8, 128)) for r in jnp.split(jnp.where(low[:4], mean, turned), 4)
    ]
    cen_z, mean_rr, mean_rp, mean_pp = [
        jnp.broadcast_to(r, (8, 128)) for r in jnp.split(jnp.where(low[:4], turned, mean), 4)
    ]
    var_rr = mean_rr - cen_x * cen_x - cen_y * cen_y
    var_rp = mean_rp - cen_x * cen_px - cen_y * cen_py
    var_pp = mean_pp - cen_px * cen_px - cen_py * cen_py
    full = counts > 0.0
    scale = jnp.where(full, inverse * (population / (2.0 * kick_scale * math.log(2.0))), 0.0)
    scale_sq = (-2.0 * math.log(2.0)) * scale * scale
    half_z = 0.5 * cen_z
    cen = jnp.where(low, cen_x, cen_y)
    cen_p = jnp.where(low, cen_px, cen_py)
    first = jnp.where(low, 0, 2)
    zero = jnp.zeros((8, 128), jnp.float32)
    place = jnp.where(row == first, scale, zero)
    place = jnp.where(row == first + 1, -scale * half_z, place)
    place = jnp.where(row == 4, -0.5 * scale * cen_p, place)
    place = jnp.where(row == 6, -scale * (cen - half_z * cen_p), place)
    quad = 0.125 * var_pp
    line = 0.5 * var_rp - 0.25 * cen_z * var_pp
    const = soft_width + 0.5 * var_rr - half_z * var_rp + 0.5 * half_z * half_z * var_pp
    width = jnp.where(row == 4, scale_sq * line, zero)
    width = jnp.where(row == 5, scale_sq * quad, width)
    width = jnp.where(row == 6, jnp.where(full, scale_sq * const, -1.0), width)
    table = jnp.concatenate([place, width], axis=1)
    high = bf(table).astype(jnp.float32)
    rest = table - high
    stacked = jnp.concatenate([high, high, rest, rest], axis=0)
    turned = jnp.transpose(stacked)
    order = [turned[j + SLICES * f : j + SLICES * f + 8] for j in range(0, SLICES, 8) for f in range(3)]
    return bf(jnp.concatenate(order, axis=0))


def kernel(
    nb, nz, population,
    part_ref, ids_ref, maps_ref, sext_ref, out_ref,
    x_in, id_in, x_out, state, tiles, id_dense, onehot, counts, mom_rows, mom_bf, kick_rows, kick_bf, kick_x, kick_y,
    send_buf, recv_buf, ahead,
    send_sem, recv_sem, load_sem, swap_send, swap_recv, out_sem, out_send, out_recv,
):
    bunches, comps, width = part_ref.shape[1:]
    half_tiles = width // 128
    ntile = 2 * half_tiles
    groups = ntile // 8
    me = lax.axis_index("bunch")
    dom = lax.axis_index("dom")
    zed, core = lax.div(dom, 2), lax.rem(dom, 2)
    other = 1 - core
    peer = (me, 2 * zed + other)

    def partner_column(distance):
        return lax.rem(me + jnp.where(core == 0, nb - distance, distance), nb)

    own_x = pltpu.make_async_copy(part_ref.at[core], x_in.at[0], load_sem.at[0])
    own_id = pltpu.make_async_copy(ids_ref.at[core], id_in.at[0], load_sem.at[1])
    own_x.start()
    own_id.start()

    barrier = pltpu.get_barrier_semaphore()
    pl.semaphore_signal(barrier, inc=1, device_id=peer, device_id_type=MESH)

    def greet(k, carry):
        column = partner_column(lax.rem(k + 1, nb))
        for r in range(nz):
            pl.semaphore_signal(barrier, inc=1, device_id=(column, 2 * r + other), device_id_type=MESH)
        return carry

    lax.fori_loop(0, SECTIONS, greet, 0)
    swap_x = pltpu.make_async_remote_copy(
        src_ref=part_ref.at[other], dst_ref=x_in.at[1], send_sem=swap_send.at[0], recv_sem=swap_recv.at[0],
        device_id=peer, device_id_type=MESH,
    )
    swap_id = pltpu.make_async_remote_copy(
        src_ref=ids_ref.at[other], dst_ref=id_in.at[1], send_sem=swap_send.at[1], recv_sem=swap_recv.at[1],
        device_id=peer, device_id_type=MESH,
    )
    slot_id = (lax.broadcasted_iota(jnp.int32, (128, 128), 1) & (SLICES - 1)).astype(jnp.float32)
    parts = groups // 2

    def take(h):
        first = h * half_tiles

        def unpack(i, carry):
            for t in range(half_tiles):
                tiles[pl.ds((first + t) * 8, comps), :] = x_in[h, i, :, 128 * t : 128 * (t + 1)]
            for c in range(comps):
                for g in range(h * parts, (h + 1) * parts):
                    state[i, c, 8 * g : 8 * g + 8, :] = tiles[pl.ds(64 * g + c, 8, stride=8), :]
            return carry

        def build(i, carry):
            columns = jnp.transpose(id_dense[i])
            for t in range(first, first + half_tiles):
                onehot[i, 128 * t : 128 * (t + 1), :] = bf(jnp.where(columns[:, t : t + 1] == slot_id, 1.0, 0.0))
            return carry

        lax.fori_loop(0, bunches, unpack, 0)
        for t in range(half_tiles):
            tiles[pl.ds((first + t) * 8, bunches), :] = id_in[h, :, 128 * t : 128 * (t + 1)].astype(jnp.float32)
        for i in range(bunches):
            for g in range(h * parts, (h + 1) * parts):
                id_dense[i, 8 * g : 8 * g + 8, :] = tiles[pl.ds(64 * g + i, 8, stride=8), :]
        lax.fori_loop(0, bunches, build, 0)

    own_x.wait()
    own_id.wait()
    for i in range(bunches):
        id_dense[i] = jnp.zeros((ntile, 128), jnp.float32)
    take(0)
    pl.semaphore_wait(barrier, SECTIONS * nz + 1)
    swap_id.start()
    swap_x.start()
    mom_bf[...] = jnp.ones(mom_bf.shape, jnp.bfloat16)
    swap_id.wait()
    swap_x.wait()
    take(1)

    def count(i, carry):
        counts[i] = jnp.dot(mom_bf[...], onehot[i], preferred_element_type=jnp.float32)[:8]
        return carry

    lax.fori_loop(0, bunches, count, 0)
    for g in range(groups):
        kick_rows[pl.ds(64 * g + 7, 8, stride=8), :] = jnp.zeros((8, 128), jnp.float32)
    low = lax.broadcasted_iota(jnp.int32, (8, 128), 1) < SLICES
    one = jnp.ones((8, 128), jnp.float32)

    def cells(step):
        base = (core * SECTIONS + lax.rem(step, SECTIONS)) * comps * comps
        return [[maps_ref[base + comps * r + c] for c in range(comps)] for r in range(comps)]

    def prepare(step, i):
        cell = cells(step)
        for g in range(groups):
            rows = slice(8 * g, 8 * g + 8)
            old = [state[i, c, rows, :] for c in range(comps)]
            for r in range(comps):
                total = cell[r][0] * old[0]
                for c in range(1, comps):
                    total = total + cell[r][c] * old[c]
                ahead[r, rows, :] = total

    def gathered(ref, g):
        total = ref[pl.ds(64 * g, 8, stride=8), :]
        for r in range(1, 8):
            total = total + ref[pl.ds(64 * g + r, 8, stride=8), :]
        return total

    def advance(step, i, kicked):
        cell = cells(step)
        strength = sext_ref[core, lax.rem(step, SECTIONS)]
        for g in range(groups):
            rows = slice(8 * g, 8 * g + 8)
            new = [ahead[r, rows, :] for r in range(comps)]
            if kicked:
                add_x, add_y = gathered(kick_x, g), gathered(kick_y, g)
                new = [new[r] + (cell[r][1] * add_x + cell[r][3] * add_y) for r in range(comps)]
            x, px, y, py, z, dp = new
            xx, yy = x * x, y * y
            px = px + strength * (xx - yy)
            py = py - 2.0 * strength * (x * y)
            for c, value in enumerate((x, px, y, py, z, dp)):
                state[i, c, rows, :] = value
            half = 0.5 * z
            mom = (x, px, y, py, z, xx + yy, x * px + y * py, px * px + py * py)
            kick = (x + half * px, px, y + half * py, py, z, z * z, one)
            for f, value in enumerate(mom):
                mom_rows[pl.ds(64 * g + f, 8, stride=8), :] = value
            for f, value in enumerate(kick):
                kick_rows[pl.ds(64 * g + f, 8, stride=8), :] = value
        for t in range(ntile):
            mom_bf[:, 128 * t : 128 * (t + 1)] = split_rows(mom_rows[8 * t : 8 * t + 8, :])
        sums = jnp.dot(mom_bf[...], onehot[i], preferred_element_type=jnp.float32)
        sums = sums[:8] + sums[8:]
        send_buf[step * bunches + i] = jnp.concatenate(
            [jnp.where(low[:4], sums[:4], sums[4:]), counts[i, :4, :]], axis=0
        )

    def features(i):
        for t in range(ntile):
            kick_bf[i, :, 128 * t : 128 * (t + 1)] = split_rows(kick_rows[8 * t : 8 * t + 8, :])

    def send(step, i):
        n = step * bunches + i
        column = partner_column(lax.rem(lax.rem(step, SECTIONS) + 1, nb))
        for r in sorted(range(nz), key=lambda r: -min(r, nz - r)):
            pltpu.make_async_remote_copy(
                src_ref=send_buf.at[n, pl.ds(0, ROWS)], dst_ref=recv_buf.at[n, zed, pl.ds(0, ROWS)],
                send_sem=send_sem.at[n], recv_sem=recv_sem.at[n],
                device_id=(column, 2 * lax.rem(zed + r, nz) + other), device_id_type=MESH,
            ).start()

    def meet(step, i):
        n = step * bunches + i
        landed = recv_buf.at[n, :, pl.ds(0, ROWS)]
        pltpu.make_async_copy(landed, landed, recv_sem.at[n]).wait()
        sums = recv_buf[n, 0, :ROWS]
        for r in range(1, nz):
            sums = sums + recv_buf[n, r, :ROWS]
        return slice_coefficients(sums, population)

    def chunk(table, i, m):
        part = kick_bf[i, :, CHUNK * m : CHUNK * (m + 1)]
        made = jnp.dot(table, jnp.concatenate([part, part], axis=0), preferred_element_type=jnp.float32)
        for u in range(CHUNK // 128):
            lanes = slice(128 * u, 128 * (u + 1))
            total_x = total_y = None
            for j in range(0, SLICES, 8):
                dx = made[3 * j : 3 * j + 8, lanes]
                dy = made[3 * j + 8 : 3 * j + 16, lanes]
                recip = 1.0 / made[3 * j + 16 : 3 * j + 24, lanes]
                factor = jnp.exp2((dx * dx + dy * dy) * recip) * recip
                total_x = factor * dx if j == 0 else total_x + factor * dx
                total_y = factor * dy if j == 0 else total_y + factor * dy
            row = (m * (CHUNK // 128) + u) * 8
            kick_x[row : row + 8, :] = total_x
            kick_y[row : row + 8, :] = total_y

    def slot(step, i):
        table = meet(step, i)
        for m in range(ntile * 128 // CHUNK):
            chunk(table, i, m)

    for i in range(bunches):
        prepare(0, i)
        advance(0, i, False)
        send(0, i)
        features(i)

    def cycle(step, carry):
        for i in range(bunches):
            prepare(step + 1, i)
            slot(step, i)
            advance(step + 1, i, True)
            send(step + 1, i)
            features(i)
        return carry

    lax.fori_loop(0, STEPS - 1, cycle, 0)

    def own_out(i):
        return pltpu.make_async_copy(x_out.at[0, i], out_ref.at[core, i], out_sem.at[i])

    def swap_out(i):
        return pltpu.make_async_remote_copy(
            src_ref=x_out.at[1, i], dst_ref=out_ref.at[core, i], send_sem=out_send.at[i], recv_sem=out_recv.at[i],
            device_id=peer, device_id_type=MESH,
        )

    for i in range(bunches):
        slot(STEPS - 1, i)
        for c in range(comps):
            for g in range(groups):
                value = state[i, c, 8 * g : 8 * g + 8, :]
                if c in (1, 3):
                    value = value + gathered(kick_x if c == 1 else kick_y, g)
                tiles[pl.ds(64 * g + c, 8, stride=8), :] = value
        for h in range(2):
            for t in range(half_tiles):
                x_out[h, i, :, 128 * t : 128 * (t + 1)] = tiles[pl.ds((h * half_tiles + t) * 8, comps), :]
        own_out(i).start()
        swap_out(i).start()

    def finish(i, carry):
        own_out(i).wait()
        swap_out(i).wait()
        return carry

    def drain(n, carry):
        landed = recv_buf.at[n, :, pl.ds(0, ROWS)]
        pltpu.make_async_copy(landed, landed, send_sem.at[n]).wait()
        return carry

    lax.fori_loop(0, STEPS * bunches, drain, 0)
    lax.fori_loop(0, bunches, finish, 0)


def body(particles, slice_ids, maps, sextupoles):
    nb, nd = lax.axis_size("bunch"), lax.axis_size("dom")
    nz = nd // 2
    beams, bunches, comps, width = particles.shape
    ntile = 2 * width // 128
    slots = STEPS * bunches
    f32, b16 = jnp.float32, jnp.bfloat16
    vmem, dma = pltpu.VMEM, pltpu.SemaphoreType.DMA
    return pl.pallas_call(
        functools.partial(kernel, nb, nz, float(width * nd)),
        out_shape=jax.ShapeDtypeStruct(particles.shape, f32),
        in_specs=[
            pl.BlockSpec(memory_space=pltpu.HBM),
            pl.BlockSpec(memory_space=pltpu.HBM),
            pl.BlockSpec(memory_space=pltpu.SMEM),
            pl.BlockSpec(memory_space=pltpu.SMEM),
        ],
        out_specs=pl.BlockSpec(memory_space=pl.ANY),
        scratch_shapes=[
            vmem((2, bunches, comps, width), f32),
            vmem((2, bunches, width), jnp.int32),
            vmem((2, bunches, comps, width), f32),
            vmem((bunches, comps, ntile, 128), f32),
            vmem((8 * ntile + 8, 128), f32),
            vmem((bunches, ntile, 128), f32),
            vmem((bunches, 2 * width, 128), b16),
            vmem((bunches, 8, 128), f32),
            vmem((8 * ntile + 8, 128), f32),
            vmem((16, 2 * width), b16),
            vmem((8 * ntile + 8, 128), f32),
            vmem((bunches, 16, 2 * width), b16),
            vmem((8 * ntile + 8, 128), f32),
            vmem((8 * ntile + 8, 128), f32),
            vmem((slots, 8, 128), f32),
            vmem((slots, nz, 8, 128), f32),
            vmem((comps, ntile, 128), f32),
            dma((slots,)),
            dma((slots,)),
            dma((2,)),
            dma((2,)),
            dma((2,)),
            dma((bunches,)),
            dma((bunches,)),
            dma((bunches,)),
        ],
        compiler_params=pltpu.CompilerParams(
            collective_id=0, has_side_effects=True, vmem_limit_bytes=40 << 20
        ),
        name="track",
    )(particles, slice_ids, maps.reshape(-1), sextupoles)


def solution(mesh):
    return jax.shard_map(
        body,
        mesh=mesh,
        in_specs=(P(None, "bunch", None, "dom"), P(None, "bunch", "dom"), P(), P()),
        out_specs=P(None, "bunch", None, "dom"),
        check_vma=False,
    )
```
